32 devices in a mesh: pages: 2 (over y), tile: 8 (over z, x), mp: 2 (over core).
Axes of the slice: x: 2, y: 2, z: 4, core: 2. Of those that a mesh axis runs over, the one named last changes fastest.
Arguments:
- queries: bfloat16 [3072, 1024], P(('pages', 'tile'), 'mp'), parts along dimension 0, may hold values from -10.5 to 10.5
- key_rows: bfloat16 [3072, 1024], P(('pages', 'tile'), 'mp'), parts along dimension 0, may hold values from -8.5 to 8.5
- value_rows: bfloat16 [3072, 1024], P(('pages', 'tile'), 'mp'), parts along dimension 0, may hold values from -6 to 6
- grad_out: bfloat16 [3072, 1024], P(('pages', 'tile'), 'mp'), parts along dimension 0, may hold values from -6 to 6
- owner_shard: int32 [3072], P(('pages', 'tile')), parts along dimension 0, may hold values from 0 to 7, as said below
- logit_scale: float32 [16], P('mp'), may hold values from 0.5 to 2
Outputs:
- grad_queries: bfloat16 [3072, 1024], P(('pages', 'tile'), 'mp'), parts along dimension 0
- grad_keys: bfloat16 [3072, 1024], P(('pages', 'tile'), 'mp'), parts along dimension 0
- grad_values: bfloat16 [3072, 1024], P(('pages', 'tile'), 'mp'), parts along dimension 0
The draws below stay inside these ranges and needn't reach their ends.
There are 2 independent parts, one for each index of `pages`. The reference program is written for one: setup_inputs(seed, part) draws one part's arguments, and reference() takes and returns one part's arrays. A program takes and returns all parts, laid end to end along the dimension named above; an argument that names none is the same for every part. Nothing has to cross between parts.
Inputs may be any that keep to these rules, and one draw needn't show every extreme that they name: `owner_shard`: the 192 tokens of one index of tile name any one region at most 48 times; in every draw one region is named exactly 48 times by the tokens of every index of tile, so it holds 384 tokens.
All inputs are finite; a program needn't handle non-finite values.
Results may differ from the reference program's by a relative error of at most 0.0035.
The reference program's roundings to bfloat16 on the way count: a program that leaves them out, or rounds other values in their place, can miss the bound.
Values may be sent and summed in bfloat16 or wider, within the bound.
A program may use at most 64 MiB of HBM per device.

```python
import math
import jax
import jax.numpy as jnp
from jax import lax

H = 16
E = 64
TOK_DEV = 192
TOKENS = 1536
SHARDS = 8
SLOT = 48
CAPACITY = 384


def draw_queries(key, part):
    base = jnp.clip(jax.random.normal(jax.random.fold_in(key, 32), (TOKENS, H * E), jnp.float32), -4.5, 4.5)
    return base.astype(jnp.bfloat16)


def draw_key_rows(key, part):
    base = jnp.clip(jax.random.normal(jax.random.fold_in(key, 34), (TOKENS, H * E), jnp.float32), -4.5, 4.5)
    return base.astype(jnp.bfloat16)


def draw_owner_shard(key, part):
    favored = jax.random.randint(jax.random.fold_in(key, 21), (), 0, SHARDS)
    pull_level = jax.random.randint(jax.random.fold_in(key, 22), (SHARDS,), 0, 3)
    noise_bits = jax.random.randint(jax.random.fold_in(key, 23), (SHARDS, SHARDS, SLOT), 0, 512)
    dest_ids = jnp.arange(SHARDS, dtype=jnp.int32)
    priority = noise_bits + 256 * pull_level[None, :, None] + 4096 * (dest_ids == favored).astype(jnp.int32)[None, :, None]
    flat_priority = priority.reshape(SHARDS, SHARDS * SLOT) * (SHARDS * SLOT) + jnp.arange(SHARDS * SLOT, dtype=jnp.int32)[None, :]
    chosen = lax.top_k(flat_priority, TOK_DEV)[1]
    dest_shard = (chosen // SLOT).astype(jnp.int32)
    order_keys = jax.random.randint(jax.random.fold_in(key, 24), (SHARDS, TOK_DEV), 0, 1 << 20) * TOK_DEV + jnp.arange(TOK_DEV, dtype=jnp.int32)[None, :]
    shuffle = jnp.argsort(order_keys, axis=1)
    mixed = jnp.take_along_axis(dest_shard, shuffle, axis=1)
    return mixed.reshape(TOKENS).astype(jnp.int32)


def block_scale(own_key, dims, shards, smallest, largest):
    gain, own = 1.0, jax.random.fold_in(own_key, 6)
    for dim, blocks in shards:
        steps = jnp.exp(jax.random.uniform(jax.random.fold_in(own, dim), (blocks,), jnp.float32, smallest / len(shards), largest / len(shards)))
        gain = gain * jnp.repeat(steps, dims[dim] // blocks).reshape([-1 if axis == dim else 1 for axis in range(len(dims))])
    return gain


def noise(key, shape, scale, most, pieces=(), held_as=jnp.bfloat16):
    entries = jax.random.normal(key, shape, jnp.float32) * scale
    if len(pieces) > 0:
        entries = block_scale(key, shape, pieces, -0.22, 0.18) * entries
    return jnp.clip(entries, min=-most, max=most).astype(held_as)


def setup_inputs(seed: int = 0, part: int = 0) -> dict:
    keys = jax.random.split(jax.random.key(seed), 7)
    own_keys = jax.random.split(jax.random.fold_in(keys[6], part), 7)
    queries = draw_queries(jax.random.fold_in(jax.random.fold_in(keys[6], part), 71), part)
    key_rows = draw_key_rows(jax.random.fold_in(jax.random.fold_in(keys[6], part), 71), part)
    value_rows = noise(own_keys[2], (TOKENS, H * E), 1.0, 6.0, ((0, 8), (1, 2)))
    grad_out = noise(own_keys[3], (TOKENS, H * E), 1.0, 6.0, ((0, 8), (1, 2)))
    owner_shard = draw_owner_shard(jax.random.fold_in(jax.random.fold_in(keys[6], part), 71), part)
    logit_scale = jnp.clip(jnp.exp(math.log(2.0) - 1.3862944 * jax.random.uniform(keys[5], (H,), jnp.float32) ** block_scale(keys[5], (H,), ((0, 2),), -0.2, 0.2)), 0.5, 2.0)
    return dict(queries=queries, key_rows=key_rows, value_rows=value_rows, grad_out=grad_out, owner_shard=owner_shard, logit_scale=logit_scale)


def attend_heads(query_heads, key_heads, value_heads, dout_heads, live_rows):
    pair_mask = live_rows[None, :, None] & live_rows[None, None, :]
    scores = jnp.einsum('ihe,jhe->hij', query_heads, key_heads, preferred_element_type=jnp.float32)
    scores = jnp.where(pair_mask, scores, -1e+30)
    row_max = lax.optimization_barrier(jnp.max(scores, axis=2, keepdims=True))
    raw_weights = jnp.where(pair_mask, jnp.exp(scores - row_max), 0.0)
    row_sum = lax.optimization_barrier(jnp.sum(raw_weights, axis=2, keepdims=True))
    row_sum = jnp.where(live_rows[None, :, None], row_sum, 1.0)
    weights = raw_weights / row_sum
    weights_low = weights.astype(jnp.bfloat16)
    attended = jnp.einsum('hij,jhe->ihe', weights_low, value_heads, preferred_element_type=jnp.float32)
    row_delta = lax.optimization_barrier(jnp.sum(dout_heads.astype(jnp.float32) * attended, axis=2))
    dprobs = jnp.einsum('ihe,jhe->hij', dout_heads, value_heads, preferred_element_type=jnp.float32)
    dscores = (weights * (dprobs - jnp.transpose(row_delta)[:, :, None])).astype(jnp.bfloat16)
    grad_value = jnp.einsum('hij,ihe->jhe', weights_low, dout_heads, preferred_element_type=jnp.float32).astype(jnp.bfloat16)
    grad_key = jnp.einsum('hij,ihe->jhe', dscores, query_heads, preferred_element_type=jnp.float32).astype(jnp.bfloat16)
    grad_raw = jnp.einsum('hij,jhe->ihe', dscores, key_heads, preferred_element_type=jnp.float32).astype(jnp.bfloat16)
    return (grad_raw, grad_key, grad_value)

def reference(queries, key_rows, value_rows, grad_out, owner_shard, logit_scale):
    scale_cols = jnp.repeat(logit_scale / math.sqrt(E), E)
    scaled = (queries.astype(jnp.float32) * scale_cols).astype(jnp.bfloat16)

    def region_step(carry, shard):
        found = jnp.nonzero(owner_shard == shard, size=CAPACITY, fill_value=TOKENS)[0].astype(jnp.int32)
        live_rows = found < TOKENS
        safe_rows = jnp.minimum(found, TOKENS - 1)

        def pick_rows(source):
            return source[safe_rows].reshape(CAPACITY, H, E)
        results = attend_heads(pick_rows(scaled), pick_rows(key_rows), pick_rows(value_rows), pick_rows(grad_out), live_rows)
        target = jnp.where(live_rows, found, TOKENS)
        updated = tuple((held.at[target].set(piece.reshape(CAPACITY, H * E).astype(held.dtype), mode='drop') for held, piece in zip(carry, results)))
        return (updated, None)
    blank = jnp.zeros((TOKENS, H * E), jnp.bfloat16)
    final, _ = lax.scan(region_step, (blank, blank, blank), jnp.arange(SHARDS, dtype=jnp.int32))
    grad_queries = (final[0].astype(jnp.float32) * scale_cols).astype(jnp.bfloat16)
    return (grad_queries, final[1], final[2])
```

```python
import functools
import math

import jax
import jax.numpy as jnp
from jax import lax
from jax.experimental import pallas as pl
from jax.experimental.pallas import tpu as pltpu
from jax.sharding import PartitionSpec as P

MESH = pl.DeviceIdType.MESH
CONTRACT_LANES = (((1,), (1,)), ((), ()))


def dot(left, right):
    return jnp.dot(left, right, preferred_element_type=jnp.float32)


def swap_halves(tile):
    return pltpu.roll(tile, tile.shape[1] // 2, 1)


def exchange_kernel(
    n,
    slot,
    head_size,
    ids_ref,
    scale_ref,
    q_ref,
    k_ref,
    v_ref,
    g_ref,
    oq_ref,
    ok_ref,
    ov_ref,
    send_place,
    send_qk,
    send_vg,
    got_place,
    got_qk,
    got_vg,
    region_qk,
    region_vg,
    bias,
    probs,
    probs_low,
    dscores,
    out_kv,
    out_q,
    ret_kv,
    ret_q,
    back_kv,
    back_q,
    send_sem,
    recv_sem,
):
    me = lax.axis_index("tile")
    tokens = q_ref.shape[0]
    capacity = n * slot
    width = 2 * head_size
    half = tokens // 2
    f32, bf16 = jnp.float32, jnp.bfloat16
    root = 1.0 / math.sqrt(head_size)

    barrier = pltpu.get_barrier_semaphore()
    for d in range(1, n):
        pl.semaphore_signal(
            barrier, inc=1, device_id={"tile": lax.rem(me + d, n)}, device_id_type=MESH
        )

    def low_lanes(rows):
        return lax.broadcasted_iota(jnp.int32, (rows, width), 1) < head_size

    low = low_lanes(tokens)
    for pair in range(n // 2):
        cols = slice(pair * width, (pair + 1) * width)
        lane_scale = jnp.where(low, scale_ref[2 * pair] * root, scale_ref[2 * pair + 1] * root)
        q = (q_ref[:, cols].astype(f32) * lane_scale).astype(bf16).astype(f32)
        k = k_ref[:, cols].astype(f32)
        v = v_ref[:, cols].astype(f32)
        g = g_ref[:, cols].astype(f32)
        send_qk[2 * pair] = jnp.where(low, q, swap_halves(k)).astype(bf16)
        send_qk[2 * pair + 1] = jnp.where(low, swap_halves(q), k).astype(bf16)
        send_vg[2 * pair] = jnp.where(low, v, swap_halves(g)).astype(bf16)
        send_vg[2 * pair + 1] = jnp.where(low, swap_halves(v), g).astype(bf16)

    ids = ids_ref[...]
    mine = (lax.broadcasted_iota(jnp.int32, (n, tokens), 0) == ids).astype(f32)
    earlier = (
        lax.broadcasted_iota(jnp.int32, (tokens, tokens), 0)
        < lax.broadcasted_iota(jnp.int32, (tokens, tokens), 1)
    ).astype(bf16)
    rank = jnp.sum(dot(mine.astype(bf16), earlier) * mine, axis=0, keepdims=True)
    send_place[...] = jnp.broadcast_to(ids.astype(f32) * slot + rank, (8, tokens))

    pl.semaphore_wait(barrier, n - 1)

    def remote(kind, d, src, dst, peer):
        copy = pltpu.make_async_remote_copy(
            src_ref=src,
            dst_ref=dst,
            send_sem=send_sem.at[kind, d],
            recv_sem=recv_sem.at[kind, d],
            device_id={"tile": peer},
            device_id_type=MESH,
        )
        copy.start()
        return copy

    order = sorted(range(1, n), key=lambda d: -min(d, n - d))
    place_copies, qk_copies, vg_copies = {}, {}, {}
    for d in order:
        peer = lax.rem(me + d, n)
        place_copies[d] = remote(0, d, send_place, got_place.at[d], peer)
        qk_copies[d] = remote(1, d, send_qk.at[peer], got_qk.at[d], peer)
    for d in order:
        peer = lax.rem(me + d, n)
        vg_copies[d] = remote(2, d, send_vg.at[peer], got_vg.at[d], peer)

    got_place[0] = send_place[...]
    arrivals = [0] + order[::-1]

    def pick(d):
        rows = lax.broadcasted_iota(jnp.int32, (capacity, tokens), 0).astype(f32)
        return (rows == got_place[d][0:1, :]).astype(bf16)

    for d in arrivals:
        if d:
            place_copies[d].wait_recv()
            qk_copies[d].wait_recv()
        block = got_qk[d] if d else send_qk[me]
        region_qk[:, d] = dot(pick(d), block).astype(bf16).reshape(n, slot, width)

    counts = jnp.zeros((n, capacity), f32)
    table = jnp.zeros((8, tokens), f32)
    slot_of = lax.broadcasted_iota(jnp.int32, (n, capacity), 1)
    region_row = lax.broadcasted_iota(jnp.int32, (n, tokens), 0).astype(f32) * slot
    for d in range(n):
        place = got_place[d]
        held = (place[0:1, :] >= region_row) & (place[0:1, :] < region_row + slot)
        count = jnp.sum(held.astype(f32), axis=1, keepdims=True)
        counts = jnp.where((slot_of >= d * slot) & (slot_of < (d + 1) * slot), count + d * slot, counts)
        table = jnp.where(lax.broadcasted_iota(jnp.int32, (8, tokens), 0) == d, place, table)
    bias_rows = jnp.where(slot_of.astype(f32) < counts, 0.0, -1e30)
    bias_cols = jnp.transpose(bias_rows)
    for r in range(n):
        bias[r] = jnp.broadcast_to(bias_cols[:, r : r + 1], (capacity, 128))
    place_cols = jnp.transpose(table)

    low_cap = low_lanes(capacity)
    blocks = [slice(b * 128, (b + 1) * 128) for b in range(capacity // 128)]

    def score_step(r, carry):
        qk = region_qk[r].reshape(capacity, width)
        key_low = jnp.where(low_cap, swap_halves(qk.astype(f32)), 0.0).astype(bf16)
        for b in blocks:
            scores = lax.dot_general(
                key_low, qk[b], CONTRACT_LANES, preferred_element_type=f32
            ) + bias[r]
            raw = jnp.exp(scores - jnp.max(scores, axis=0, keepdims=True))
            probs[r, :, b] = raw * (1.0 / jnp.sum(raw, axis=0, keepdims=True))
        return carry

    lax.fori_loop(0, n, score_step, 0)

    for d in arrivals:
        if d:
            vg_copies[d].wait_recv()
        block = got_vg[d] if d else send_vg[me]
        region_vg[:, d] = dot(pick(d), block).astype(bf16).reshape(n, slot, width)

    my_scale = scale_ref[me] * root

    def grad_step(r, carry):
        qk = region_qk[r].reshape(capacity, width)
        vg = region_vg[r].reshape(capacity, width)
        vg_wide = vg.astype(f32)
        value_low = jnp.where(low_cap, vg_wide, 0.0).astype(bf16)
        gv = swap_halves(vg_wide).astype(bf16)
        for b in blocks:
            dprobs = lax.dot_general(
                value_low, gv[b], CONTRACT_LANES, preferred_element_type=f32
            )
            weights = probs[r, :, b]
            weights_low = weights.astype(bf16)
            delta = jnp.sum(weights_low.astype(f32) * dprobs, axis=0, keepdims=True)
            probs_low[:, b] = weights_low
            dscores[:, b] = (weights * (dprobs - delta)).astype(bf16)
        grads = jnp.where(low_cap, dot(dscores[...], qk), dot(probs_low[...], vg))
        key_t = jnp.transpose(qk.astype(f32))[head_size:].astype(bf16)
        raw_t = dot(key_t, dscores[...]).astype(bf16).astype(f32) * my_scale
        raw = jnp.transpose(jnp.concatenate([raw_t, raw_t], axis=0))
        out_kv[:, r] = grads.astype(bf16).reshape(n, slot, width)
        out_q[:, r] = raw.astype(bf16).reshape(n, slot, width)
        return carry

    lax.fori_loop(0, n, grad_step, 0)

    low_half = low_lanes(half)
    back_copies = []
    for d in order + [0]:
        lanes = lax.broadcasted_iota(jnp.int32, (tokens, capacity), 1).astype(f32)
        put = (lanes == place_cols[:, d : d + 1]).astype(bf16)
        kv = dot(put, out_kv[d].reshape(capacity, width)).astype(bf16)
        gq = dot(put, out_q[d].reshape(capacity, width))
        gq = jnp.where(low_half, gq[:half], gq[half:]).astype(bf16)
        if d:
            peer = lax.rem(me + n - d, n)
            ret_kv[d] = kv
            ret_q[d] = gq
            back_copies.append(remote(3, d, ret_kv.at[d], back_kv.at[me], peer))
            back_copies.append(remote(4, d, ret_q.at[d], back_q.at[me], peer))
        else:
            back_kv[me] = kv
            back_q[me] = gq
    for copy in back_copies:
        copy.wait_recv()

    for pair in range(n // 2):
        cols = slice(pair * width, (pair + 1) * width)
        kv0, kv1 = back_kv[2 * pair].astype(f32), back_kv[2 * pair + 1].astype(f32)
        gq0, gq1 = back_q[2 * pair].astype(f32), back_q[2 * pair + 1].astype(f32)
        ok_ref[:, cols] = jnp.where(low, kv0, swap_halves(kv1)).astype(bf16)
        ov_ref[:, cols] = jnp.where(low, swap_halves(kv0), kv1).astype(bf16)
        oq_ref[:half, cols] = jnp.where(low_half, gq0, swap_halves(gq1)).astype(bf16)
        oq_ref[half:, cols] = jnp.where(low_half, swap_halves(gq0), gq1).astype(bf16)

    for copies in (place_copies, qk_copies, vg_copies):
        for copy in copies.values():
            copy.wait_send()
    for copy in back_copies:
        copy.wait_send()


def by_heads(queries, key_rows, value_rows, grad_out, owner_shard, logit_scale):
    n = lax.axis_size("tile")
    tokens, columns = queries.shape
    head_size = columns // n
    capacity = 2 * tokens
    slot = capacity // n
    width = 2 * head_size
    bf16, f32 = jnp.bfloat16, jnp.float32
    vmem = pl.BlockSpec(memory_space=pltpu.VMEM)
    smem = pl.BlockSpec(memory_space=pltpu.SMEM)
    out = jax.ShapeDtypeStruct((tokens, columns), bf16)
    return pl.pallas_call(
        functools.partial(exchange_kernel, n, slot, head_size),
        out_shape=(out, out, out),
        in_specs=[vmem, smem, vmem, vmem, vmem, vmem],
        out_specs=(vmem, vmem, vmem),
        scratch_shapes=[
            pltpu.VMEM((8, tokens), f32),
            pltpu.VMEM((n, tokens, width), bf16),
            pltpu.VMEM((n, tokens, width), bf16),
            pltpu.VMEM((n, 8, tokens), f32),
            pltpu.VMEM((n, tokens, width), bf16),
            pltpu.VMEM((n, tokens, width), bf16),
            pltpu.VMEM((n, n, slot, width), bf16),
            pltpu.VMEM((n, n, slot, width), bf16),
            pltpu.VMEM((n, capacity, 128), f32),
            pltpu.VMEM((n, capacity, capacity), f32),
            pltpu.VMEM((capacity, capacity), bf16),
            pltpu.VMEM((capacity, capacity), bf16),
            pltpu.VMEM((n, n, slot, width), bf16),
            pltpu.VMEM((n, n, slot, width), bf16),
            pltpu.VMEM((n, tokens, width), bf16),
            pltpu.VMEM((n, tokens // 2, width), bf16),
            pltpu.VMEM((n, tokens, width), bf16),
            pltpu.VMEM((n, tokens // 2, width), bf16),
            pltpu.SemaphoreType.DMA((5, n)),
            pltpu.SemaphoreType.DMA((5, n)),
        ],
        compiler_params=pltpu.CompilerParams(
            collective_id=0, has_side_effects=True, vmem_limit_bytes=56 * 1024 * 1024
        ),
    )(owner_shard.reshape(1, tokens), logit_scale, queries, key_rows, value_rows, grad_out)


def attend_heads(query_heads, key_heads, value_heads, dout_heads, live_rows):
    pair_mask = live_rows[None, :, None] & live_rows[None, None, :]
    scores = jnp.einsum("ihe,jhe->hij", query_heads, key_heads, preferred_element_type=jnp.float32)
    scores = jnp.where(pair_mask, scores, -1e30)
    row_max = jnp.max(scores, axis=2, keepdims=True)
    raw_weights = jnp.where(pair_mask, jnp.exp(scores - row_max), 0.0)
    row_sum = jnp.sum(raw_weights, axis=2, keepdims=True)
    row_sum = jnp.where(live_rows[None, :, None], row_sum, 1.0)
    weights = raw_weights / row_sum
    weights_low = weights.astype(jnp.bfloat16)
    attended = jnp.einsum(
        "hij,jhe->ihe", weights_low, value_heads, preferred_element_type=jnp.float32
    )
    row_delta = jnp.sum(dout_heads.astype(jnp.float32) * attended, axis=2)
    dprobs = jnp.einsum("ihe,jhe->hij", dout_heads, value_heads, preferred_element_type=jnp.float32)
    dscores = (weights * (dprobs - jnp.transpose(row_delta)[:, :, None])).astype(jnp.bfloat16)
    grad_value = jnp.einsum(
        "hij,ihe->jhe", weights_low, dout_heads, preferred_element_type=jnp.float32
    ).astype(jnp.bfloat16)
    grad_key = jnp.einsum(
        "hij,ihe->jhe", dscores, query_heads, preferred_element_type=jnp.float32
    ).astype(jnp.bfloat16)
    grad_raw = jnp.einsum(
        "hij,jhe->ihe", dscores, key_heads, preferred_element_type=jnp.float32
    ).astype(jnp.bfloat16)
    return (grad_raw, grad_key, grad_value)


def attend_items(query_items, key_items, value_items, dout_items, live_rows):
    capacity = query_items.shape[0]
    item_count = query_items.shape[1]
    head_size = query_items.shape[2] // 2
    outputs = ([], [], [])
    for item_index in range(item_count):
        halves = ([], [], [])
        for half_index in range(2):
            lower = half_index * head_size
            upper = lower + head_size
            pieces = attend_heads(
                query_items[:, item_index, lower:upper].reshape(capacity, 1, head_size),
                key_items[:, item_index, lower:upper].reshape(capacity, 1, head_size),
                value_items[:, item_index, lower:upper].reshape(capacity, 1, head_size),
                dout_items[:, item_index, lower:upper].reshape(capacity, 1, head_size),
                live_rows,
            )
            for holder, piece in zip(halves, pieces):
                holder.append(piece.reshape(capacity, head_size))
        for holder, parts_list in zip(outputs, halves):
            holder.append(jnp.concatenate(parts_list, axis=1))
    return tuple((jnp.stack(holder, axis=1) for holder in outputs))


def slot_places(owner_shard, shards, slot):
    one_hot = (owner_shard[:, None] == jnp.arange(shards, dtype=jnp.int32)[None, :]).astype(
        jnp.int32
    )
    before = jnp.cumsum(one_hot, axis=0) - one_hot
    rank = jnp.sum(before * one_hot, axis=1)
    return owner_shard * slot + rank


def by_regions(queries, key_rows, value_rows, grad_out, owner_shard, logit_scale):
    shards = lax.axis_size("tile")
    tok_rows, columns = queries.shape
    heads_here = logit_scale.shape[0]
    head_size = columns // heads_here
    capacity = 2 * tok_rows
    slot = capacity // shards
    pairs = heads_here // 2
    width = 2 * head_size
    slot_index = slot_places(owner_shard, shards, slot)
    scale_cols = jnp.repeat(logit_scale / math.sqrt(head_size), head_size)
    scaled = (queries.astype(jnp.float32) * scale_cols).astype(jnp.bfloat16)

    def spread(source):
        return jnp.zeros((capacity,) + source.shape[1:], source.dtype).at[slot_index].set(source)

    sent_query = spread(scaled)
    sent_key = spread(key_rows)
    sent_value = spread(value_rows)
    sent_dout = spread(grad_out)
    flags = spread(jnp.ones((tok_rows,), jnp.int32))
    got_query, got_key, got_value, got_dout, got_flags = (
        lax.all_to_all(sent_query, "tile", split_axis=0, concat_axis=0, tiled=True),
        lax.all_to_all(sent_key, "tile", split_axis=0, concat_axis=0, tiled=True),
        lax.all_to_all(sent_value, "tile", split_axis=0, concat_axis=0, tiled=True),
        lax.all_to_all(sent_dout, "tile", split_axis=0, concat_axis=0, tiled=True),
        lax.all_to_all(flags, "tile", split_axis=0, concat_axis=0, tiled=True),
    )
    grad_raw, grad_key, grad_value = attend_items(
        got_query.reshape(capacity, pairs, width),
        got_key.reshape(capacity, pairs, width),
        got_value.reshape(capacity, pairs, width),
        got_dout.reshape(capacity, pairs, width),
        got_flags > 0,
    )
    returned = (
        lax.all_to_all(
            grad_raw.reshape(capacity, columns), "tile", split_axis=0, concat_axis=0, tiled=True
        ),
        lax.all_to_all(
            grad_key.reshape(capacity, columns), "tile", split_axis=0, concat_axis=0, tiled=True
        ),
        lax.all_to_all(
            grad_value.reshape(capacity, columns), "tile", split_axis=0, concat_axis=0, tiled=True
        ),
    )
    grad_queries = (returned[0][slot_index].astype(jnp.float32) * scale_cols).astype(jnp.bfloat16)
    return (grad_queries, returned[1][slot_index], returned[2][slot_index])


def local(queries, key_rows, value_rows, grad_out, owner_shard, logit_scale):
    shards = lax.axis_size("tile")
    tokens, columns = queries.shape
    heads_here = logit_scale.shape[0]
    slot = 2 * tokens // shards
    fits = (
        shards == heads_here == 8
        and columns == heads_here * 64
        and slot % 16 == 0
        and (2 * tokens) % 128 == 0
        and tokens % 32 == 0
    )
    plan = by_heads if fits else by_regions
    return plan(queries, key_rows, value_rows, grad_out, owner_shard, logit_scale)


def solution(mesh):
    return jax.shard_map(
        local,
        mesh=mesh,
        in_specs=(
            P(("pages", "tile"), "mp"),
            P(("pages", "tile"), "mp"),
            P(("pages", "tile"), "mp"),
            P(("pages", "tile"), "mp"),
            P(("pages", "tile")),
            P("mp"),
        ),
        out_specs=(
            P(("pages", "tile"), "mp"),
            P(("pages", "tile"), "mp"),
            P(("pages", "tile"), "mp"),
        ),
        check_vma=False,
    )
```

```python
import functools
import math

import jax
import jax.numpy as jnp
from jax import lax
from jax.experimental import pallas as pl
from jax.experimental.pallas import tpu as pltpu
from jax.sharding import PartitionSpec as P

MESH = pl.DeviceIdType.MESH
CONTRACT_LANES = (((1,), (1,)), ((), ()))


def dot(left, right):
    return jnp.dot(left, right, preferred_element_type=jnp.float32)


def swap_halves(tile):
    return pltpu.roll(tile, tile.shape[1] // 2, 1)


def exchange_kernel(
    n,
    slot,
    head_size,
    ids_ref,
    scale_ref,
    q_hbm,
    k_hbm,
    v_hbm,
    g_hbm,
    back_kq,
    back_v,
    q_ref,
    k_ref,
    v_ref,
    g_ref,
    send_place,
    send_qk,
    send_g,
    send_v,
    got_place,
    got_qk,
    got_g,
    got_v,
    region_qk,
    region_k,
    region_kt,
    region_g,
    region_v,
    bias,
    probs,
    probs_low,
    dscores,
    out_v,
    out_kq,
    ret_v,
    ret_kq,
    load_sem,
    send_sem,
    recv_sem,
):
    me = lax.axis_index("tile")
    tokens = q_ref.shape[0]
    capacity = n * slot
    width = 2 * head_size
    half = tokens // 2
    f32, bf16 = jnp.float32, jnp.bfloat16
    root = 1.0 / math.sqrt(head_size)

    barrier = pltpu.get_barrier_semaphore()
    for d in range(1, n):
        pl.semaphore_signal(
            barrier, inc=1, device_id={"tile": lax.rem(me + d, n)}, device_id_type=MESH
        )
    loads = [
        pltpu.make_async_copy(src, dst, load_sem.at[i])
        for i, (src, dst) in enumerate(
            ((q_hbm, q_ref), (k_hbm, k_ref), (g_hbm, g_ref), (v_hbm, v_ref))
        )
    ]
    for load in loads:
        load.start()

    def low_lanes(rows):
        return lax.broadcasted_iota(jnp.int32, (rows, width), 1) < head_size

    ids = ids_ref[...]
    mine = (lax.broadcasted_iota(jnp.int32, (n, tokens), 0) == ids).astype(f32)
    earlier = (
        lax.broadcasted_iota(jnp.int32, (tokens, tokens), 0)
        < lax.broadcasted_iota(jnp.int32, (tokens, tokens), 1)
    ).astype(bf16)
    rank = jnp.sum(dot(mine.astype(bf16), earlier) * mine, axis=0, keepdims=True)
    send_place[...] = jnp.broadcast_to(ids.astype(f32) * slot + rank, (8, tokens))

    low, low_half, low_cap = low_lanes(tokens), low_lanes(half), low_lanes(capacity)
    pairs = [
        (2 * pair, 2 * pair + 1, slice(pair * width, (pair + 1) * width))
        for pair in range(n // 2)
    ]
    loads[0].wait()
    loads[1].wait()
    for one, two, cols in pairs:
        lane_scale = jnp.where(low, scale_ref[one] * root, scale_ref[two] * root)
        q = (q_ref[:, cols].astype(f32) * lane_scale).astype(bf16).astype(f32)
        k = k_ref[:, cols].astype(f32)
        send_qk[one] = jnp.where(low, q, swap_halves(k)).astype(bf16)
        send_qk[two] = jnp.where(low, swap_halves(q), k).astype(bf16)

    pl.semaphore_wait(barrier, n - 1)

    def remote(kind, d, src, dst, peer):
        copy = pltpu.make_async_remote_copy(
            src_ref=src,
            dst_ref=dst,
            send_sem=send_sem.at[kind, d],
            recv_sem=recv_sem.at[kind, d],
            device_id={"tile": peer},
            device_id_type=MESH,
        )
        copy.start()
        return copy

    order = sorted(range(1, n), key=lambda d: -min(d, n - d))
    arrivals = [0] + order[::-1]
    place_copies, qk_copies, g_copies, v_copies = {}, {}, {}, {}
    for d in order:
        peer = lax.rem(me + d, n)
        place_copies[d] = remote(0, d, send_place, got_place.at[d], peer)
        qk_copies[d] = remote(1, d, send_qk.at[peer], got_qk.at[d], peer)

    def fold(ref, send, load):
        load.wait()
        for one, two, cols in pairs:
            top, bottom = ref[:half, cols].astype(f32), ref[half:, cols].astype(f32)
            send[one] = jnp.where(low_half, top, swap_halves(bottom)).astype(bf16)
            send[two] = jnp.where(low_half, swap_halves(top), bottom).astype(bf16)

    fold(g_ref, send_g, loads[2])
    fold(v_ref, send_v, loads[3])

    for d in order:
        peer = lax.rem(me + d, n)
        qk_copies[d].wait_send()
        g_copies[d] = remote(2, d, send_g.at[peer], got_g.at[d], peer)

    got_place[0] = send_place[...]

    def pick(d):
        rows = lax.broadcasted_iota(jnp.int32, (capacity, tokens), 0).astype(f32)
        return (rows == got_place[d][0:1, :]).astype(bf16)

    for d in arrivals:
        if d:
            place_copies[d].wait_recv()
            qk_copies[d].wait_recv()
        block = got_qk[d] if d else send_qk[me]
        placed = dot(pick(d), block)
        key_low = jnp.where(low_cap, swap_halves(placed), 0.0)
        region_qk[:, d] = placed.astype(bf16).reshape(n, slot, width)
        region_k[:, d] = key_low.astype(bf16).reshape(n, slot, width)

    counts = jnp.zeros((n, capacity), f32)
    table = jnp.zeros((8, tokens), f32)
    slot_of = lax.broadcasted_iota(jnp.int32, (n, capacity), 1)
    region_row = lax.broadcasted_iota(jnp.int32, (n, tokens), 0).astype(f32) * slot
    for d in range(n):
        place = got_place[d]
        held = (place[0:1, :] >= region_row) & (place[0:1, :] < region_row + slot)
        count = jnp.sum(held.astype(f32), axis=1, keepdims=True)
        here = (slot_of >= d * slot) & (slot_of < (d + 1) * slot)
        counts = jnp.where(here, count + d * slot, counts)
        table = jnp.where(lax.broadcasted_iota(jnp.int32, (8, tokens), 0) == d, place, table)
    bias_cols = jnp.transpose(jnp.where(slot_of.astype(f32) < counts, 0.0, -1e30))
    for r in range(n):
        bias[r] = jnp.broadcast_to(bias_cols[:, r : r + 1], (capacity, 128))
    place_cols = jnp.transpose(table)

    blocks = [slice(b * 128, (b + 1) * 128) for b in range(capacity // 128)]

    def score_step(r, carry):
        qk = region_qk[r].reshape(capacity, width)
        key_low = region_k[r].reshape(capacity, width)
        for b in blocks:
            scores = lax.dot_general(
                key_low, qk[b], CONTRACT_LANES, preferred_element_type=f32
            ) + bias[r]
            raw = jnp.exp(scores - jnp.max(scores, axis=0, keepdims=True))
            weights = raw * (1.0 / jnp.sum(raw, axis=0, keepdims=True))
            probs[r, :, b] = weights
            probs_low[r, :, b] = weights.astype(bf16)
        region_kt[r] = jnp.transpose(qk.astype(f32))[head_size:].astype(bf16)
        return carry

    lax.fori_loop(0, n, score_step, 0, unroll=n // 2)

    for d in order:
        peer = lax.rem(me + d, n)
        g_copies[d].wait_send()
        v_copies[d] = remote(3, d, send_v.at[peer], got_v.at[d], peer)

    def unfold(got, send, d):
        folded = (got[d] if d else send[me]).astype(f32)
        return jnp.concatenate([folded, swap_halves(folded)], axis=0).astype(bf16)

    for d in arrivals:
        if d:
            g_copies[d].wait_recv()
        placed = dot(pick(d), unfold(got_g, send_g, d))
        region_g[:, d] = placed.astype(bf16).reshape(n, slot, width)

    def value_step(r, carry):
        grads = dot(probs_low[r], region_g[r].reshape(capacity, width))
        out_v[:, r] = grads.astype(bf16).reshape(n, slot, width)
        return carry

    lax.fori_loop(0, n, value_step, 0, unroll=n // 2)

    def put(d, source):
        lanes = lax.broadcasted_iota(jnp.int32, (tokens, capacity), 1).astype(f32)
        rows = (lanes == place_cols[:, d : d + 1]).astype(bf16)
        return dot(rows, source[d].reshape(capacity, width))

    back_copies = []
    for d in order + [0]:
        grads = put(d, out_v)
        grads = jnp.where(low_half, grads[:half], swap_halves(grads[half:])).astype(bf16)
        if d:
            ret_v[d] = grads
            peer = lax.rem(me + n - d, n)
            back_copies.append(remote(4, d, ret_v.at[d], back_v.at[me], peer))
        else:
            back_v[me] = grads

    for d in arrivals:
        if d:
            v_copies[d].wait_recv()
        placed = jnp.where(low_cap, dot(pick(d), unfold(got_v, send_v, d)), 0.0)
        region_v[:, d] = placed.astype(bf16).reshape(n, slot, width)

    my_scale = scale_ref[me] * root

    def grad_step(r, carry):
        value_low = region_v[r].reshape(capacity, width)
        g = region_g[r].reshape(capacity, width)
        for b in blocks:
            dprobs = lax.dot_general(
                value_low, g[b], CONTRACT_LANES, preferred_element_type=f32
            )
            delta = jnp.sum(
                probs_low[r, :, b].astype(f32) * dprobs, axis=0, keepdims=True
            )
            dscores[r, :, b] = (probs[r, :, b] * (dprobs - delta)).astype(bf16)
        grads = dot(dscores[r], region_qk[r].reshape(capacity, width))
        raw_t = dot(region_kt[r], dscores[r]).astype(bf16).astype(f32) * my_scale
        raw = jnp.transpose(jnp.concatenate([raw_t, raw_t], axis=0))
        grads = jnp.where(low_cap, grads, raw)
        out_kq[:, r] = grads.astype(bf16).reshape(n, slot, width)
        return carry

    lax.fori_loop(0, n, grad_step, 0, unroll=n // 2)

    for d in order + [0]:
        grads = put(d, out_kq).astype(bf16)
        if d:
            ret_kq[d] = grads
            peer = lax.rem(me + n - d, n)
            back_copies.append(remote(5, d, ret_kq.at[d], back_kq.at[me], peer))
        else:
            back_kq[me] = grads
    for copy in back_copies:
        copy.wait_recv()
    for copies in (place_copies, v_copies):
        for copy in copies.values():
            copy.wait_send()
    for copy in back_copies:
        copy.wait_send()


def unpack_kernel(n, kq_ref, v_ref, oq_ref, ok_ref, ov_ref):
    tokens, width = kq_ref.shape[1:]
    half = tokens // 2
    f32, bf16 = jnp.float32, jnp.bfloat16
    low = lax.broadcasted_iota(jnp.int32, (tokens, width), 1) < width // 2
    low_half = lax.broadcasted_iota(jnp.int32, (half, width), 1) < width // 2
    for pair in range(n // 2):
        cols = slice(pair * width, (pair + 1) * width)
        kq0, kq1 = kq_ref[2 * pair].astype(f32), kq_ref[2 * pair + 1].astype(f32)
        v0, v1 = v_ref[2 * pair].astype(f32), v_ref[2 * pair + 1].astype(f32)
        ok_ref[:, cols] = jnp.where(low, kq0, swap_halves(kq1)).astype(bf16)
        oq_ref[:, cols] = jnp.where(low, swap_halves(kq0), kq1).astype(bf16)
        ov_ref[:half, cols] = jnp.where(low_half, v0, swap_halves(v1)).astype(bf16)
        ov_ref[half:, cols] = jnp.where(low_half, swap_halves(v0), v1).astype(bf16)


def by_heads(queries, key_rows, value_rows, grad_out, owner_shard, logit_scale):
    n = lax.axis_size("tile")
    tokens, columns = queries.shape
    head_size = columns // n
    capacity = 2 * tokens
    slot = capacity // n
    width = 2 * head_size
    bf16, f32 = jnp.bfloat16, jnp.float32
    vmem = pl.BlockSpec(memory_space=pltpu.VMEM)
    smem = pl.BlockSpec(memory_space=pltpu.SMEM)
    anywhere = pl.BlockSpec(memory_space=pltpu.HBM)
    full = pltpu.VMEM((n, tokens, width), bf16)
    folded = pltpu.VMEM((n, tokens // 2, width), bf16)
    region = pltpu.VMEM((n, n, slot, width), bf16)
    square = (n, capacity, capacity)
    grant = 67043328 - 3 * n * tokens * width - 64 * 1024
    back_kq, back_v = pl.pallas_call(
        functools.partial(exchange_kernel, n, slot, head_size),
        out_shape=(
            pltpu.VMEM((n, tokens, width), bf16),
            pltpu.VMEM((n, tokens // 2, width), bf16),
        ),
        in_specs=[vmem, smem, anywhere, anywhere, anywhere, anywhere],
        out_specs=(vmem, vmem),
        scratch_shapes=[pltpu.VMEM((tokens, columns), bf16)] * 4
        + [pltpu.VMEM((8, tokens), f32), full, folded, folded]
        + [pltpu.VMEM((n, 8, tokens), f32), full, folded, folded]
        + [region, region, pltpu.VMEM((n, head_size, capacity), bf16), region, region]
        + [pltpu.VMEM((n, capacity, 128), f32), pltpu.VMEM(square, f32)]
        + [pltpu.VMEM(square, bf16), pltpu.VMEM(square, bf16)]
        + [region, region, folded, full]
        + [pltpu.SemaphoreType.DMA((4,))]
        + [pltpu.SemaphoreType.DMA((6, n))] * 2,
        compiler_params=pltpu.CompilerParams(
            collective_id=0, has_side_effects=True, vmem_limit_bytes=grant
        ),
    )(owner_shard.reshape(1, tokens), logit_scale, queries, key_rows, value_rows, grad_out)
    out = jax.ShapeDtypeStruct((tokens, columns), bf16)
    return pl.pallas_call(
        functools.partial(unpack_kernel, n),
        out_shape=(out, out, out),
        in_specs=[vmem, vmem],
        out_specs=(vmem, vmem, vmem),
        compiler_params=pltpu.CompilerParams(vmem_limit_bytes=8 * 1024 * 1024),
    )(back_kq, back_v)


def attend_heads(query_heads, key_heads, value_heads, dout_heads, live_rows):
    pair_mask = live_rows[None, :, None] & live_rows[None, None, :]
    scores = jnp.einsum("ihe,jhe->hij", query_heads, key_heads, preferred_element_type=jnp.float32)
    scores = jnp.where(pair_mask, scores, -1e30)
    row_max = jnp.max(scores, axis=2, keepdims=True)
    raw_weights = jnp.where(pair_mask, jnp.exp(scores - row_max), 0.0)
    row_sum = jnp.sum(raw_weights, axis=2, keepdims=True)
    row_sum = jnp.where(live_rows[None, :, None], row_sum, 1.0)
    weights = raw_weights / row_sum
    weights_low = weights.astype(jnp.bfloat16)
    attended = jnp.einsum(
        "hij,jhe->ihe", weights_low, value_heads, preferred_element_type=jnp.float32
    )
    row_delta = jnp.sum(dout_heads.astype(jnp.float32) * attended, axis=2)
    dprobs = jnp.einsum("ihe,jhe->hij", dout_heads, value_heads, preferred_element_type=jnp.float32)
    dscores = (weights * (dprobs - jnp.transpose(row_delta)[:, :, None])).astype(jnp.bfloat16)
    grad_value = jnp.einsum(
        "hij,ihe->jhe", weights_low, dout_heads, preferred_element_type=jnp.float32
    ).astype(jnp.bfloat16)
    grad_key = jnp.einsum(
        "hij,ihe->jhe", dscores, query_heads, preferred_element_type=jnp.float32
    ).astype(jnp.bfloat16)
    grad_raw = jnp.einsum(
        "hij,jhe->ihe", dscores, key_heads, preferred_element_type=jnp.float32
    ).astype(jnp.bfloat16)
    return (grad_raw, grad_key, grad_value)


def attend_items(query_items, key_items, value_items, dout_items, live_rows):
    capacity = query_items.shape[0]
    item_count = query_items.shape[1]
    head_size = query_items.shape[2] // 2
    outputs = ([], [], [])
    for item_index in range(item_count):
        halves = ([], [], [])
        for half_index in range(2):
            lower = half_index * head_size
            upper = lower + head_size
            pieces = attend_heads(
                query_items[:, item_index, lower:upper].reshape(capacity, 1, head_size),
                key_items[:, item_index, lower:upper].reshape(capacity, 1, head_size),
                value_items[:, item_index, lower:upper].reshape(capacity, 1, head_size),
                dout_items[:, item_index, lower:upper].reshape(capacity, 1, head_size),
                live_rows,
            )
            for holder, piece in zip(halves, pieces):
                holder.append(piece.reshape(capacity, head_size))
        for holder, parts_list in zip(outputs, halves):
            holder.append(jnp.concatenate(parts_list, axis=1))
    return tuple((jnp.stack(holder, axis=1) for holder in outputs))


def slot_places(owner_shard, shards, slot):
    one_hot = (owner_shard[:, None] == jnp.arange(shards, dtype=jnp.int32)[None, :]).astype(
        jnp.int32
    )
    before = jnp.cumsum(one_hot, axis=0) - one_hot
    rank = jnp.sum(before * one_hot, axis=1)
    return owner_shard * slot + rank


def by_regions(queries, key_rows, value_rows, grad_out, owner_shard, logit_scale):
    shards = lax.axis_size("tile")
    tok_rows, columns = queries.shape
    heads_here = logit_scale.shape[0]
    head_size = columns // heads_here
    capacity = 2 * tok_rows
    slot = capacity // shards
    pairs = heads_here // 2
    width = 2 * head_size
    slot_index = slot_places(owner_shard, shards, slot)
    scale_cols = jnp.repeat(logit_scale / math.sqrt(head_size), head_size)
    scaled = (queries.astype(jnp.float32) * scale_cols).astype(jnp.bfloat16)

    def spread(source):
        return jnp.zeros((capacity,) + source.shape[1:], source.dtype).at[slot_index].set(source)

    sent_query = spread(scaled)
    sent_key = spread(key_rows)
    sent_value = spread(value_rows)
    sent_dout = spread(grad_out)
    flags = spread(jnp.ones((tok_rows,), jnp.int32))
    got_query, got_key, got_value, got_dout, got_flags = (
        lax.all_to_all(sent_query, "tile", split_axis=0, concat_axis=0, tiled=True),
        lax.all_to_all(sent_key, "tile", split_axis=0, concat_axis=0, tiled=True),
        lax.all_to_all(sent_value, "tile", split_axis=0, concat_axis=0, tiled=True),
        lax.all_to_all(sent_dout, "tile", split_axis=0, concat_axis=0, tiled=True),
        lax.all_to_all(flags, "tile", split_axis=0, concat_axis=0, tiled=True),
    )
    grad_raw, grad_key, grad_value = attend_items(
        got_query.reshape(capacity, pairs, width),
        got_key.reshape(capacity, pairs, width),
        got_value.reshape(capacity, pairs, width),
        got_dout.reshape(capacity, pairs, width),
        got_flags > 0,
    )
    returned = (
        lax.all_to_all(
            grad_raw.reshape(capacity, columns), "tile", split_axis=0, concat_axis=0, tiled=True
        ),
        lax.all_to_all(
            grad_key.reshape(capacity, columns), "tile", split_axis=0, concat_axis=0, tiled=True
        ),
        lax.all_to_all(
            grad_value.reshape(capacity, columns), "tile", split_axis=0, concat_axis=0, tiled=True
        ),
    )
    grad_queries = (returned[0][slot_index].astype(jnp.float32) * scale_cols).astype(jnp.bfloat16)
    return (grad_queries, returned[1][slot_index], returned[2][slot_index])


def local(queries, key_rows, value_rows, grad_out, owner_shard, logit_scale):
    shards = lax.axis_size("tile")
    tokens, columns = queries.shape
    heads_here = logit_scale.shape[0]
    slot = 2 * tokens // shards
    fits = (
        shards == heads_here == 8
        and columns == heads_here * 64
        and slot % 16 == 0
        and (2 * tokens) % 128 == 0
        and tokens % 32 == 0
    )
    plan = by_heads if fits else by_regions
    return plan(queries, key_rows, value_rows, grad_out, owner_shard, logit_scale)


def solution(mesh):
    return jax.shard_map(
        local,
        mesh=mesh,
        in_specs=(
            P(("pages", "tile"), "mp"),
            P(("pages", "tile"), "mp"),
            P(("pages", "tile"), "mp"),
            P(("pages", "tile"), "mp"),
            P(("pages", "tile")),
            P("mp"),
        ),
        out_specs=(
            P(("pages", "tile"), "mp"),
            P(("pages", "tile"), "mp"),
            P(("pages", "tile"), "mp"),
        ),
        check_vma=False,
    )
```
